256 devices in a mesh: section: 2 (over y_lo), dp: 4 (over y_hi, core), shard: 32 (over x, z).
Axes of the slice: x: 4, y: 4 (y_hi: 2, y_lo: 2; y = y_hi * 2 + y_lo), z: 8, core: 2. Of those that a mesh axis runs over, the one named last changes fastest.
Arguments:
- norm_input: bfloat16 [2, 4, 4096, 3584], P('section', 'dp', 'shard'), may hold values from -6 to 6
- norm_gain: float32 [2, 3584], P('section'), may hold values from 0.1 to 1.9
- branch_grad: bfloat16 [2, 4, 4096, 3584], P('section', 'dp', 'shard'), may hold values from -6 to 6
- residual_grad: bfloat16 [2, 4, 4096, 3584], P('section', 'dp', 'shard'), may hold values from -6 to 6
- down_weight: bfloat16 [2, 14336, 3584], P('section', 'shard'), may hold values from -0.09375 to 0.09375
Outputs:
- boundary_grad: bfloat16 [2, 4, 4096, 3584], P('section', 'dp', 'shard')
- gain_grad: float32 [2, 3584], P('section')
- unit_grads: bfloat16 [2, 4, 4096, 14336], P('section', 'dp', None, 'shard')
The draws below stay inside these ranges and needn't reach their ends.
All inputs are finite; a program needn't handle non-finite values.
Results may differ from the reference program's by a relative error of at most 0.0049.
Values may be sent and summed in bfloat16 or wider, within the bound.
A program may use at most 128 MiB of HBM per device.

```python
import jax
import jax.numpy as jnp
from jax import lax

D = 3584
SEQ = 4096
FF = 14336
BATCH = 4
SECTIONS = 2


def block_levels(key, dims, shards, smallest, top_value):
    gain, own = 1.0, jax.random.fold_in(key, 6)
    for position, shards_of in shards:
        heights = jnp.exp(jax.random.uniform(jax.random.fold_in(own, position), (shards_of,), jnp.float32, smallest / len(shards), top_value / len(shards)))
        gain = gain * jnp.repeat(heights, dims[position] // shards_of).reshape([-1 if axis == position else 1 for axis in range(len(dims))])
    return gain


def noise(rng, dims, width, most, split=(), dtype=jnp.bfloat16):
    loudness = block_levels(rng, dims, split, -0.22, 0.18) if split else 1.0
    entries = jax.random.normal(rng, dims, jnp.float32) * width * loudness
    return jnp.minimum(jnp.maximum(entries, -most), most).astype(dtype)


def setup_inputs(seed: int = 0) -> dict:
    key_list = jax.random.split(jax.random.key(seed), 6)
    norm_input = noise(key_list[0], (SECTIONS, BATCH, SEQ, D), 1.0, 6.0, ((0, 2), (1, 4), (2, 32)))
    norm_gain = jnp.clip(1.0 + 0.18 * jax.random.normal(key_list[1], (SECTIONS, D), jnp.float32), 0.1, 1.9)
    branch_grad = noise(key_list[2], (SECTIONS, BATCH, SEQ, D), 1.0, 6.0, ((0, 2), (1, 4), (2, 32)))
    residual_grad = noise(key_list[3], (SECTIONS, BATCH, SEQ, D), 1.0, 6.0, ((0, 2), (1, 4), (2, 32)))
    down_weight = noise(key_list[4], (SECTIONS, FF, D), D ** -0.5, 0.09375, ((0, 2), (1, 32)))
    return dict(norm_input=norm_input, norm_gain=norm_gain, branch_grad=branch_grad, residual_grad=residual_grad, down_weight=down_weight)


epsilon = 1e-05

def reference(norm_input, norm_gain, branch_grad, residual_grad, down_weight):
    values = norm_input.astype(jnp.float32)
    inverse = lax.rsqrt(lax.optimization_barrier(jnp.mean(values * values, axis=-1, keepdims=True)) + epsilon)
    normed = values * inverse
    upstream = branch_grad.astype(jnp.float32)
    scaled = upstream * norm_gain[:, None, None, :]
    project = lax.optimization_barrier(jnp.mean(scaled * normed, axis=-1, keepdims=True))
    boundary = (residual_grad.astype(jnp.float32) + inverse * (scaled - normed * project)).astype(jnp.bfloat16)
    gain_grad = lax.optimization_barrier(jnp.sum(upstream * normed, axis=(1, 2))) / SEQ
    arrived = jnp.flip(boundary, axis=0).astype(jnp.float32)
    unit_grads = jnp.einsum('gbsd,ghd->gbsh', arrived, down_weight.astype(jnp.float32), precision=lax.Precision.HIGHEST).astype(jnp.bfloat16)
    return (boundary, gain_grad, unit_grads)
```

```python
import functools

import jax
import jax.numpy as jnp
from jax import lax
from jax.experimental import pallas as pl
from jax.experimental.pallas import tpu as pltpu
from jax.sharding import Mesh
from jax.sharding import PartitionSpec as P

DP_SHARD = ("dp_0", "dp_1", "shard_0", "shard_1")
SHARD = ("shard_0", "shard_1")
DP = ("dp_0", "dp_1")
MESH = pl.DeviceIdType.MESH

epsilon = 1e-05

CHUNKS = 4


def wrap(axis, offset):
    size = lax.axis_size(axis)
    return {axis: lax.rem(lax.axis_index(axis) + (offset % size), size)}


def flip(axis, bit):
    me = lax.axis_index(axis)
    return {axis: me + bit - 2 * bit * lax.rem(me // bit, 2)}


def first_row(rows, hop, way):
    if hop == 0:
        return 0
    if hop == 4:
        return 7 * rows
    return rows * (1 + 2 * (hop - 1) + way)


def kernel(

    input_ref,
    gain_ref,
    branch_ref,
    residual_ref,
    weight_ref,
    boundary_out,
    gain_out,
    unit_out,
    values,
    branch,
    residual,
    boundary,
    acts,
    weight,
    result,
    gain_sum,
    gain_in,
    load_sem,
    own_weight_sem,
    boundary_sem,
    own_result_sem,
    section_send,
    section_recv,
    ring_send,
    ring_recv,
    row_send,
    row_recv,
    core_send,
    core_recv,
    twin_send,
    twin_recv,
    result_send,
    result_recv,
    gain_send,
    gain_recv,
):
    rows, features = input_ref.shape
    units = weight_ref.shape[0]
    quarter = units // 4
    step = rows // CHUNKS
    me_x = lax.axis_index("shard_0")
    me_z = lax.axis_index("shard_1")
    me_twin = lax.axis_index("dp_0")
    me_core = lax.axis_index("dp_1")

    right, left = wrap("shard_1", 1), wrap("shard_1", -1)
    up, down = wrap("shard_0", 1), wrap("shard_0", -1)
    partner, twin, core = wrap("section", 1), wrap("dp_0", 1), wrap("dp_1", 1)
    gain_partners = (
        core,
        twin,
        flip("shard_0", 1),
        wrap("shard_0", 2),
        flip("shard_1", 1),
        flip("shard_1", 2),
        wrap("shard_1", 4),
    )

    def remote(source, target, send, receive, device):
        return pltpu.make_async_remote_copy(
            src_ref=source,
            dst_ref=target,
            send_sem=send,
            recv_sem=receive,
            device_id=device,
            device_id_type=MESH,
        )

    def load(chunk):
        span = pl.ds(pl.multiple_of(chunk * step, step), step)
        return [
            pltpu.make_async_copy(
                ref.at[span], buffer.at[span], load_sem.at[i, chunk]
            )
            for i, (ref, buffer) in enumerate(
                ((input_ref, values), (branch_ref, branch), (residual_ref, residual))
            )
        ]

    @pl.loop(0, CHUNKS)
    def _(chunk):
        for copy in load(chunk):
            copy.start()

    own_weight = pltpu.make_async_copy(weight_ref, weight.at[0], own_weight_sem)
    own_weight.start()

    barrier = pltpu.get_barrier_semaphore()
    others = (
        right,
        left,
        flip("shard_1", 2),
        wrap("shard_1", 4),
        up,
        down,
        wrap("shard_0", 2),
        partner,
        twin,
        core,
    )
    for other in others:
        pl.semaphore_signal(barrier, inc=1, device_id=other, device_id_type=MESH)
    pl.semaphore_wait(barrier, len(others))

    mine = pl.ds(
        pl.multiple_of(me_twin * (2 * quarter) + me_core * quarter, 16), quarter
    )
    theirs = pl.ds(
        pl.multiple_of((1 - me_twin) * (2 * quarter) + me_core * quarter, 16), quarter
    )

    def row_copy(i, source, target, device):
        return remote(source, target, row_send.at[i], row_recv.at[i], device)

    to_up = row_copy(0, weight_ref.at[mine], weight.at[3, mine], up)
    to_down = row_copy(1, weight_ref.at[theirs], weight.at[1, theirs], down)
    pass_up = row_copy(2, weight.at[3, mine], weight.at[2, mine], up)
    pass_down = row_copy(3, weight.at[1, theirs], weight.at[2, theirs], down)
    to_up.start()
    to_down.start()

    def same_place(i, slot, span, device, send, receive):
        piece = weight.at[slot, span]
        return remote(piece, piece, send.at[i], receive.at[i], device)

    to_core = functools.partial(
        same_place, device=core, send=core_send, receive=core_recv
    )
    core_copies = (
        to_core(0, 3, mine),
        to_core(1, 1, theirs),
        to_core(2, 2, mine),
        to_core(3, 2, theirs),
        to_core(4, 3, theirs),
        to_core(5, 1, mine),
    )
    to_twin = functools.partial(
        same_place, device=twin, send=twin_send, receive=twin_recv
    )
    twin_copies = (to_twin(0, 3, mine), to_twin(1, 1, theirs))

    def section_copy(chunk):
        span = pl.ds(pl.multiple_of(chunk * step, step), step)
        return remote(
            boundary.at[span],
            acts.at[span],
            section_send.at[chunk],
            section_recv.at[chunk],
            partner,
        )

    gain_sum[0] = jnp.zeros_like(gain_sum[0])

    @pl.loop(0, CHUNKS)
    def _(chunk):
        for copy in load(chunk):
            copy.wait()
        span = pl.ds(pl.multiple_of(chunk * step, step), step)
        x = values[span, :].astype(jnp.float32)
        inverse = lax.rsqrt(jnp.mean(x * x, axis=-1, keepdims=True) + epsilon)
        normed = x * inverse
        upstream = branch[span, :].astype(jnp.float32)
        scaled = upstream * gain_ref[...]
        project = jnp.mean(scaled * normed, axis=-1, keepdims=True)
        boundary[span, :] = (
            residual[span, :].astype(jnp.float32)
            + inverse * (scaled - normed * project)
        ).astype(boundary.dtype)
        section_copy(chunk).start()
        gain_sum[0] += jnp.sum(upstream * normed, axis=0, keepdims=True)

    boundary_copy = pltpu.make_async_copy(boundary, boundary_out, boundary_sem)
    boundary_copy.start()

    def gain_copy(i):
        return remote(
            gain_sum.at[i],
            gain_in.at[i],
            gain_send.at[i],
            gain_recv.at[i],
            gain_partners[i],
        )

    def gain_step(i):
        gain_copy(i).wait_recv()
        gain_sum[i + 1] = gain_sum[i] + gain_in[i]
        if i + 1 < len(gain_partners):
            gain_copy(i + 1).start()

    gain_copy(0).start()

    def ring_copy(way, hop, chunk):
        here = first_row(rows, hop - 1, way) + chunk * step
        there = first_row(rows, hop, way) + chunk * step
        return remote(
            acts.at[pl.ds(here, step)],
            acts.at[pl.ds(there, step)],
            ring_send.at[way, hop - 1, chunk],
            ring_recv.at[way, hop - 1, chunk],
            (right, left)[way],
        )

    def on_ring(way, hop, chunk):
        return hop < 4 or (hop == 4 and chunk % 2 == way)

    def from_section(chunk):
        section_copy(chunk).wait_recv()
        for way in range(2):
            ring_copy(way, 1, chunk).start()

    def from_ring(hop, chunk):
        for way in range(2):
            if on_ring(way, hop, chunk):
                ring_copy(way, hop, chunk).wait_recv()
                if on_ring(way, hop + 1, chunk):
                    ring_copy(way, hop + 1, chunk).start()

    def tokens_of(origin):
        return pl.ds(pl.multiple_of(me_x * (8 * rows) + origin * rows, rows), rows)

    def result_copy(block, d, origin):
        return remote(
            result.at[d, block],
            unit_out.at[:, tokens_of(origin)],
            result_send.at[d - 1, block],
            result_recv.at[d - 1, block],
            {"shard_0": lax.rem(me_x + d, 4)},
        )

    def own_result_copy(block, origin):
        return pltpu.make_async_copy(
            result.at[0, block],
            unit_out.at[:, tokens_of(origin)],
            own_result_sem.at[block],
        )

    def origins(hop):
        if hop == 0:
            return ((0, me_z),)
        if hop == 4:
            return ((7, lax.rem(me_z + 4, 8)),)
        return (
            (2 * hop - 1, lax.rem(me_z + 8 - hop, 8)),
            (2 * hop, lax.rem(me_z + hop, 8)),
        )

    def product(hop, d):
        blocks = origins(hop)
        found = lax.dot_general(
            weight[d],
            acts[pl.ds(blocks[0][0] * rows, rows * len(blocks)), :],
            (((1,), (1,)), ((), ())),
            preferred_element_type=jnp.float32,
        ).astype(result.dtype)
        for i, (block, _) in enumerate(blocks):
            result[d, block] = found[:, i * rows : (i + 1) * rows]
        return blocks

    def own_product(hop):
        for block, origin in product(hop, 0):
            own_result_copy(block, origin).start()

    def sent_product(hop, d):
        for block, origin in product(hop, d):
            result_copy(block, d, origin).start()

    def side_products(hop):
        @pl.loop(0, 2)
        def _(i):
            sent_product(hop, 1 + 2 * i)

    from_section(0)
    from_section(1)
    gain_step(0)
    from_ring(1, 0)
    from_section(2)
    own_weight.wait()
    from_ring(1, 1)
    to_up.wait_recv()
    pass_up.start()
    core_copies[0].start()
    to_down.wait_recv()
    pass_down.start()
    core_copies[1].start()
    from_section(3)
    twin_copies[0].start()
    twin_copies[1].start()
    gain_step(1)
    own_product(0)
    from_ring(1, 2)
    gain_step(2)
    from_ring(1, 3)
    own_product(1)
    gain_step(3)
    from_ring(2, 0)
    gain_step(4)
    pass_up.wait_recv()
    core_copies[2].start()
    pass_down.wait_recv()
    core_copies[3].start()
    from_ring(2, 1)
    core_copies[2].wait_recv()
    core_copies[3].wait_recv()
    sent_product(0, 2)
    sent_product(1, 2)
    from_ring(2, 2)
    gain_step(5)
    from_ring(2, 3)
    sent_product(2, 2)
    own_product(2)
    gain_step(6)
    gain_out[...] = gain_sum[7] * (1.0 / (32 * rows))
    from_ring(3, 0)
    for i in range(2):
        twin_copies[i].wait_recv()
        core_copies[4 + i].start()
    for i in (0, 1, 4, 5):
        core_copies[i].wait_recv()
    side_products(0)
    from_ring(3, 1)
    side_products(1)
    from_ring(3, 2)
    side_products(2)
    from_ring(3, 3)
    sent_product(3, 2)
    side_products(3)
    own_product(3)
    for chunk in range(CHUNKS):
        from_ring(4, chunk)
    sent_product(4, 2)
    side_products(4)
    own_product(4)

    to_up.wait_send()
    to_down.wait_send()
    pass_up.wait_send()
    pass_down.wait_send()
    for copy in core_copies + twin_copies:
        copy.wait_send()
    for i in range(len(gain_partners)):
        gain_copy(i).wait_send()
    boundary_copy.wait()

    @pl.loop(0, CHUNKS)
    def _(chunk):
        section_copy(chunk).wait_send()

    for way in range(2):
        for hop in range(1, 5):
            for chunk in range(CHUNKS):
                if on_ring(way, hop, chunk):
                    ring_copy(way, hop, chunk).wait_send()
    for hop in range(5):
        for block, origin in origins(hop):
            own_result_copy(block, origin).wait()

    @pl.loop(0, 8)
    def _(block):
        for d in (2, 1, 3):
            copy = result_copy(block, d, 0)
            copy.wait_send()
            copy.wait_recv()


def per_device(norm_input, norm_gain, branch_grad, residual_grad, down_weight):
    rows, features = norm_input.shape[2:]
    units = down_weight.shape[1]
    anywhere = pl.BlockSpec(memory_space=pl.ANY)
    whole = pl.BlockSpec(memory_space=pltpu.VMEM)
    dma = pltpu.SemaphoreType.DMA
    block = pltpu.VMEM((rows, features), jnp.bfloat16)
    boundary, gain_grad, unit_grads = pl.pallas_call(
        kernel,
        out_shape=(
            jax.ShapeDtypeStruct((rows, features), jnp.bfloat16),
            jax.ShapeDtypeStruct((1, features), jnp.float32),
            jax.ShapeDtypeStruct((units, 32 * rows), jnp.bfloat16),
        ),
        in_specs=[anywhere, whole, anywhere, anywhere, anywhere],
        out_specs=(anywhere, whole, anywhere),
        scratch_shapes=[
            block,
            block,
            block,
            block,
            pltpu.VMEM((8 * rows, features), jnp.bfloat16),
            pltpu.VMEM((4, units, features), jnp.bfloat16),
            pltpu.VMEM((4, 8, units, rows), jnp.bfloat16),
            pltpu.VMEM((8, 1, features), jnp.float32),
            pltpu.VMEM((7, 1, features), jnp.float32),
            dma((3, CHUNKS)),
            dma,
            dma,
            dma((8,)),
            dma((CHUNKS,)),
            dma((CHUNKS,)),
            dma((2, 4, CHUNKS)),
            dma((2, 4, CHUNKS)),
            dma((4,)),
            dma((4,)),
            dma((6,)),
            dma((6,)),
            dma((2,)),
            dma((2,)),
            dma((3, 8)),
            dma((3, 8)),
            dma((7,)),
            dma((7,)),
        ],
        compiler_params=pltpu.CompilerParams(
            collective_id=0, has_side_effects=True, vmem_limit_bytes=56 << 20
        ),
        cost_estimate=pl.CostEstimate(
            flops=2 * 8 * rows * 4 * units * features,
            bytes_accessed=16 << 20,
            transcendentals=rows,
        ),
        name="relay_backward",
    )(
        norm_input[0, 0],
        norm_gain,
        branch_grad[0, 0],
        residual_grad[0, 0],
        down_weight[0],
    )
    return (boundary[None, None], gain_grad, unit_grads.T[None, None])


def solution(mesh):
    split = Mesh(
        mesh.devices.reshape(mesh.shape["section"], 2, 2, 4, 8),
        ("section", "dp_0", "dp_1", "shard_0", "shard_1"),
    )
    return jax.shard_map(
        per_device,
        mesh=split,
        in_specs=(
            P("section", DP, SHARD, None),
            P("section", None),
            P("section", DP, SHARD, None),
            P("section", DP, SHARD, None),
            P("section", SHARD, None),
        ),
        out_specs=(
            P("section", DP, SHARD, None),
            P("section", None),
            P("section", DP, None, SHARD),
        ),
        check_vma=False,
    )
```

```python
import functools

import jax
import jax.numpy as jnp
from jax import lax
from jax.experimental import pallas as pl
from jax.experimental.pallas import tpu as pltpu
from jax.sharding import Mesh
from jax.sharding import PartitionSpec as P

DP_SHARD = ("dp_0", "dp_1", "shard_0", "shard_1")
SHARD = ("shard_0", "shard_1")
DP = ("dp_0", "dp_1")
MESH = pl.DeviceIdType.MESH

epsilon = 1e-05

CHUNKS = 8


def wrap(axis, offset):
    size = lax.axis_size(axis)
    return {axis: lax.rem(lax.axis_index(axis) + (offset % size), size)}


def flip(axis, bit):
    me = lax.axis_index(axis)
    return {axis: me + bit - 2 * bit * lax.rem(me // bit, 2)}


def first_row(rows, hop, way):
    if hop == 0:
        return 0
    if hop == 4:
        return 7 * rows
    return rows * (1 + 2 * (hop - 1) + way)


def kernel(
    input_ref,
    gain_ref,
    branch_ref,
    residual_ref,
    weight_ref,
    boundary_out,
    gain_out,
    unit_out,
    values,
    branch,
    residual,
    gain,
    acts,
    weight,
    result,
    gain_sum,
    gain_in,
    load_sem,
    section_recv,
    ring_recv,
    row_recv,
    core_recv,
    twin_recv,
    result_recv,
    gain_recv,
    send_sem,
):
    rows, features = input_ref.shape
    units = weight_ref.shape[0]
    step = rows // CHUNKS
    me_x = lax.axis_index("shard_0")
    me_z = lax.axis_index("shard_1")
    me_twin = lax.axis_index("dp_0")
    me_core = lax.axis_index("dp_1")

    right, left = wrap("shard_1", 1), wrap("shard_1", -1)
    up, down = wrap("shard_0", 1), wrap("shard_0", -1)
    partner, twin, core = wrap("section", 1), wrap("dp_0", 1), wrap("dp_1", 1)
    gain_partners = (
        flip("shard_1", 1),
        flip("shard_1", 2),
        wrap("shard_1", 4),
        core,
        flip("shard_0", 1),
        wrap("shard_0", 2),
        twin,
    )
    by_ring, by_section, by_weight, by_result, by_gain = 0, 2, 3, 4, 7

    def remote(source, target, send, receive, device):
        return pltpu.make_async_remote_copy(
            src_ref=source,
            dst_ref=target,
            send_sem=send_sem.at[send],
            recv_sem=receive,
            device_id=device,
            device_id_type=MESH,
        )

    def take(like, sem):
        pltpu.make_async_copy(like, like, sem).wait()

    def load(start, size, sem):
        span = pl.ds(start, size)
        for ref, buffer in (
            (input_ref, values),
            (branch_ref, branch),
            (residual_ref, residual),
        ):
            pltpu.make_async_copy(ref.at[span], buffer.at[span], sem).start()

    load(0, step, load_sem.at[0])
    gain_load = pltpu.make_async_copy(gain_ref, gain, load_sem.at[2])
    gain_load.start()

    barrier = pltpu.get_barrier_semaphore()
    others = (
        right,
        left,
        flip("shard_1", 2),
        wrap("shard_1", 4),
        up,
        down,
        wrap("shard_0", 2),
        partner,
        twin,
        core,
    )
    for other in others:
        pl.semaphore_signal(barrier, inc=1, device_id=other, device_id_type=MESH)
    load(step, rows - step, load_sem.at[1])
    own_weight = pltpu.make_async_copy(weight_ref, weight.at[0], load_sem.at[3])
    own_weight.start()

    def norm(chunk):
        span = pl.ds(pl.multiple_of(chunk * step, step), step)
        x = values[span, :].astype(jnp.float32)
        inverse = lax.rsqrt(jnp.mean(x * x, axis=-1, keepdims=True) + epsilon)
        normed = x * inverse
        upstream = branch[span, :].astype(jnp.float32)
        scaled = upstream * gain[...]
        project = jnp.mean(scaled * normed, axis=-1, keepdims=True)
        boundary_out[span, :] = (
            residual[span, :].astype(jnp.float32)
            + inverse * (scaled - normed * project)
        ).astype(boundary_out.dtype)
        gain_sum[0] += jnp.sum(upstream * normed, axis=0, keepdims=True)

    def section_copy(chunk):
        span = pl.ds(pl.multiple_of(chunk * step, step), step)
        return remote(
            boundary_out.at[span],
            acts.at[span],
            by_section,
            section_recv.at[chunk],
            partner,
        )

    half = units // 2
    passed = half // 2
    first = (passed // 2 + 15) // 16 * 16
    more = (half // 7 // 16) * 16
    shared = passed - more

    def from_edge(side, near, far, size):
        which = me_twin + side - 2 * me_twin * side
        start = me_core * half + near + which * (far - near)
        return pl.ds(pl.multiple_of(start, 16), size)

    sides = range(2)
    parts = (0, first), (first, passed - first)
    going = [from_edge(side, 0, half - passed, passed) for side in sides]
    going_parts = [
        [from_edge(side, at, half - passed + at, size) for side in sides]
        for at, size in parts
    ]
    extra = [from_edge(side, passed, half - passed - more, more) for side in sides]
    given = [from_edge(side, 0, half - shared, shared) for side in sides]
    gotten = [from_edge(side, half - shared, 0, shared) for side in sides]
    slots = (3, 1)
    ways = (up, down)

    def from_home(i, side, span):
        return remote(
            weight_ref.at[span],
            weight.at[slots[side], span],
            by_weight,
            row_recv.at[i],
            ways[side],
        )

    def onward(i, side, span):
        return remote(
            weight.at[slots[side], span],
            weight.at[2, span],
            by_weight,
            row_recv.at[i],
            ways[side],
        )

    def same_place(slot, span, device, receive):
        there = weight.at[slot, span]
        return remote(there, there, by_weight, receive, device)

    own_copies = [
        [from_home(2 * n + side, side, going_parts[n][side]) for side in sides]
        for n in range(2)
    ]
    extra_copies = [from_home(4 + side, side, extra[side]) for side in sides]
    pass_copies = [
        [onward(6 + 2 * n + side, side, going_parts[n][side]) for side in sides]
        for n in range(2)
    ]
    core_own = [
        same_place(slots[side], going[side], core, core_recv.at[side])
        for side in sides
    ]
    core_extra = [
        same_place(slots[side], extra[side], core, core_recv.at[2 + side])
        for side in sides
    ]
    core_gotten = [
        same_place(slots[side], gotten[side], core, core_recv.at[4 + side])
        for side in sides
    ]
    core_passed = [
        [
            same_place(2, going_parts[n][side], core, core_recv.at[6 + 2 * n + side])
            for side in sides
        ]
        for n in range(2)
    ]
    twin_given = [
        same_place(slots[side], given[side], twin, twin_recv.at[side])
        for side in sides
    ]

    def gain_copy(i):
        return remote(
            gain_sum.at[i], gain_in.at[i], by_gain, gain_recv.at[i], gain_partners[i]
        )

    def gain_step(i):
        gain_copy(i).wait_recv()
        gain_sum[i + 1] = gain_sum[i] + gain_in[i]
        if i + 1 < len(gain_partners):
            gain_copy(i + 1).start()

    def ring_copy(way, hop, chunk):
        here = first_row(rows, hop - 1, way) + chunk * step
        there = first_row(rows, hop, way) + chunk * step
        return remote(
            acts.at[pl.ds(here, step)],
            acts.at[pl.ds(there, step)],
            by_ring + way,
            ring_recv.at[way, hop - 1, chunk],
            (right, left)[way],
        )

    def on_ring(way, hop, chunk):
        return hop < 4 or (hop == 4 and chunk % 2 == way)

    def from_section(chunk):
        section_copy(chunk).wait_recv()
        for way in range(2):
            ring_copy(way, 1, chunk).start()

    def from_ring(hop, *chunks):
        for chunk in chunks:
            for way in range(2):
                if on_ring(way, hop, chunk):
                    ring_copy(way, hop, chunk).wait_recv()
                    if on_ring(way, hop + 1, chunk):
                        ring_copy(way, hop + 1, chunk).start()

    def tokens_of(origin):
        return pl.ds(pl.multiple_of(me_x * (8 * rows) + origin * rows, rows), rows)

    def origins(hop):
        if hop == 0:
            return ((0, me_z),)
        if hop == 4:
            return ((7, lax.rem(me_z + 4, 8)),)
        return (
            (2 * hop - 1, lax.rem(me_z + 8 - hop, 8)),
            (2 * hop, lax.rem(me_z + hop, 8)),
        )

    def product(hop, d):
        blocks = origins(hop)
        return lax.dot_general(
            weight[d],
            acts[pl.ds(blocks[0][0] * rows, rows * len(blocks)), :],
            (((1,), (1,)), ((), ())),
            preferred_element_type=jnp.float32,
        ).astype(result.dtype)

    def own_product(hop):
        found = product(hop, 0)
        for i, (_, origin) in enumerate(origins(hop)):
            unit_out[:, tokens_of(origin)] = found[:, i * rows : (i + 1) * rows]

    def sent_product(hop, d):
        found = product(hop, d)
        for i, (block, origin) in enumerate(origins(hop)):
            result[d - 1, block] = found[:, i * rows : (i + 1) * rows]
            remote(
                result.at[d - 1, block],
                unit_out.at[:, tokens_of(origin)],
                by_result + d - 1,
                result_recv.at[d - 1],
                {"shard_0": lax.rem(me_x + d, 4)},
            ).start()

    def side_products(hop):
        @pl.loop(0, 2)
        def _(i):
            sent_product(hop, 1 + 2 * i)

    gain_sum[0] = jnp.zeros_like(gain_sum[0])
    take(acts.at[pl.ds(0, 3 * step)], load_sem.at[0])
    gain_load.wait()
    norm(0)
    pl.semaphore_wait(barrier, len(others))
    section_copy(0).start()
    for copy in own_copies[0] + own_copies[1]:
        copy.start()
    take(acts.at[pl.ds(0, 3 * (rows - step))], load_sem.at[1])

    @pl.loop(1, CHUNKS)
    def _(chunk):
        norm(chunk)
        section_copy(chunk).start()

    gain_copy(0).start()

    for chunk in range(3):
        from_section(chunk)
    gain_step(0)
    from_section(3)
    from_section(4)
    for side in sides:
        own_copies[0][side].wait_recv()
        pass_copies[0][side].start()
    gain_step(1)
    from_section(5)
    from_section(6)
    from_section(7)
    for side in sides:
        own_copies[1][side].wait_recv()
        pass_copies[1][side].start()
        extra_copies[side].start()
        core_own[side].start()
        twin_given[side].start()
    from_ring(1, 0, 1, 2, 3, 4, 5)
    gain_step(2)
    from_ring(1, 6, 7)
    own_weight.wait()
    own_product(0)
    own_product(1)
    gain_step(3)
    for side in sides:
        pass_copies[0][side].wait_recv()
        core_passed[0][side].start()
    from_ring(2, 0, 1, 2)
    for side in sides:
        pass_copies[1][side].wait_recv()
        core_passed[1][side].start()
    from_ring(2, 3)
    for side in sides:
        core_passed[0][side].wait_recv()
        core_passed[1][side].wait_recv()
    sent_product(0, 2)
    sent_product(1, 2)
    from_ring(2, 4, 5)
    for side in sides:
        extra_copies[side].wait_recv()
        core_extra[side].start()
    gain_step(4)
    from_ring(2, 6, 7)
    sent_product(2, 2)
    for side in sides:
        twin_given[side].wait_recv()
        core_gotten[side].start()
    own_product(2)
    for side in sides:
        core_own[side].wait_recv()
        core_extra[side].wait_recv()
        core_gotten[side].wait_recv()
    side_products(0)
    from_ring(3, 0)
    side_products(1)
    from_ring(3, 1)
    side_products(2)
    gain_step(5)
    from_ring(3, 2, 3, 4, 5, 6, 7)
    sent_product(3, 2)
    side_products(3)
    own_product(3)
    gain_step(6)
    gain_out[...] = gain_sum[7] * (1.0 / (32 * rows))
    from_ring(4, *range(CHUNKS))
    sent_product(4, 2)
    side_products(4)
    own_product(4)

    take(gain_in, send_sem.at[by_gain])
    take(acts.at[pl.ds(0, rows)], send_sem.at[by_section])
    for way in range(2):
        take(acts.at[pl.ds(0, 3 * rows + rows // 2)], send_sem.at[by_ring + way])
    take(weight.at[pl.ds(0, 3)], send_sem.at[by_weight])
    for d in (1, 2, 3):
        take(result.at[d - 1], send_sem.at[by_result + d - 1])
        take(result.at[d - 1], result_recv.at[d - 1])


def per_device(norm_input, norm_gain, branch_grad, residual_grad, down_weight):
    rows, features = norm_input.shape[2:]
    units = down_weight.shape[1]
    anywhere = pl.BlockSpec(memory_space=pl.ANY)
    whole = pl.BlockSpec(memory_space=pltpu.VMEM)
    dma = pltpu.SemaphoreType.DMA
    block = pltpu.VMEM((rows, features), jnp.bfloat16)
    boundary, gain_grad, unit_grads = pl.pallas_call(
        kernel,
        out_shape=(
            block,
            pltpu.VMEM((1, features), jnp.float32),
            pltpu.VMEM((units, 32 * rows), jnp.bfloat16),
        ),
        in_specs=[anywhere] * 5,
        out_specs=(whole,) * 3,
        scratch_shapes=[
            block,
            block,
            block,
            pltpu.VMEM((1, features), jnp.float32),
            pltpu.VMEM((8 * rows, features), jnp.bfloat16),
            pltpu.VMEM((4, units, features), jnp.bfloat16),
            pltpu.VMEM((3, 8, units, rows), jnp.bfloat16),
            pltpu.VMEM((8, 1, features), jnp.float32),
            pltpu.VMEM((7, 1, features), jnp.float32),
            dma((4,)),
            dma((CHUNKS,)),
            dma((2, 4, CHUNKS)),
            dma((10,)),
            dma((10,)),
            dma((2,)),
            dma((3,)),
            dma((7,)),
            dma((8,)),
        ],
        compiler_params=pltpu.CompilerParams(
            collective_id=0, has_side_effects=True, vmem_limit_bytes=54 << 20
        ),
        cost_estimate=pl.CostEstimate(
            flops=2 * 8 * rows * 4 * units * features,
            bytes_accessed=16 << 20,
            transcendentals=rows,
        ),
        name="relay_backward",
    )(
        norm_input[0, 0],
        norm_gain,
        branch_grad[0, 0],
        residual_grad[0, 0],
        down_weight[0],
    )
    return (boundary[None, None], gain_grad, unit_grads.T[None, None])


def solution(mesh):
    split = Mesh(
        mesh.devices.reshape(mesh.shape["section"], 2, 2, 4, 8),
        ("section", "dp_0", "dp_1", "shard_0", "shard_1"),
    )
    return jax.shard_map(
        per_device,
        mesh=split,
        in_specs=(
            P("section", DP, SHARD, None),
            P("section", None),
            P("section", DP, SHARD, None),
            P("section", DP, SHARD, None),
            P("section", SHARD, None),
        ),
        out_specs=(
            P("section", DP, SHARD, None),
            P("section", None),
            P("section", DP, None, SHARD),
        ),
        check_vma=False,
    )
```

```python
import functools

import jax
import jax.numpy as jnp
from jax import lax
from jax.experimental import pallas as pl
from jax.experimental.pallas import tpu as pltpu
from jax.sharding import Mesh
from jax.sharding import PartitionSpec as P

DP_SHARD = ("dp_0", "dp_1", "shard_0", "shard_1")
SHARD = ("shard_0", "shard_1")
DP = ("dp_0", "dp_1")
MESH = pl.DeviceIdType.MESH

epsilon = 1e-05

CHUNKS = 8


def wrap(axis, offset):
    size = lax.axis_size(axis)
    return {axis: lax.rem(lax.axis_index(axis) + (offset % size), size)}


def flip(axis, bit):
    me = lax.axis_index(axis)
    return {axis: me + bit - 2 * bit * lax.rem(me // bit, 2)}


def first_row(rows, hop, way):
    if hop == 0:
        return 0
    if hop == 4:
        return 7 * rows
    return rows * (1 + 2 * (hop - 1) + way)


def kernel(
    input_ref,
    gain_ref,
    branch_ref,
    residual_ref,
    weight_ref,
    boundary_out,
    gain_out,
    unit_out,
    values,
    branch,
    residual,
    gain,
    acts,
    weight,
    result,
    gain_sum,
    gain_in,
    load_sem,
    section_recv,
    ring_recv,
    row_recv,
    core_recv,
    twin_recv,
    result_recv,
    gain_recv,
    send_sem,
):
    rows, features = input_ref.shape
    units = weight_ref.shape[0]
    step = rows // CHUNKS
    me_x = lax.axis_index("shard_0")
    me_z = lax.axis_index("shard_1")
    me_twin = lax.axis_index("dp_0")
    me_core = lax.axis_index("dp_1")

    right, left = wrap("shard_1", 1), wrap("shard_1", -1)
    up, down = wrap("shard_0", 1), wrap("shard_0", -1)
    partner, twin, core = wrap("section", 1), wrap("dp_0", 1), wrap("dp_1", 1)
    gain_partners = (
        flip("shard_1", 1),
        flip("shard_1", 2),
        wrap("shard_1", 4),
        core,
        flip("shard_0", 1),
        wrap("shard_0", 2),
        twin,
    )
    by_ring, by_section, by_weight, by_result, by_gain = 0, 2, 3, 4, 7

    def remote(source, target, send, receive, device):
        return pltpu.make_async_remote_copy(
            src_ref=source,
            dst_ref=target,
            send_sem=send_sem.at[send],
            recv_sem=receive,
            device_id=device,
            device_id_type=MESH,
        )

    def take(like, sem):
        pltpu.make_async_copy(like, like, sem).wait()

    def load(start, size, sem):
        span = pl.ds(start, size)
        for ref, buffer in (
            (input_ref, values),
            (branch_ref, branch),
            (residual_ref, residual),
        ):
            pltpu.make_async_copy(ref.at[span], buffer.at[span], sem).start()

    load(0, step, load_sem.at[0])
    gain_load = pltpu.make_async_copy(gain_ref, gain, load_sem.at[2])
    gain_load.start()

    barrier = pltpu.get_barrier_semaphore()
    others = (
        right,
        left,
        flip("shard_1", 2),
        wrap("shard_1", 4),
        up,
        down,
        wrap("shard_0", 2),
        partner,
        twin,
        core,
    )
    for other in others:
        pl.semaphore_signal(barrier, inc=1, device_id=other, device_id_type=MESH)
    load(step, rows - step, load_sem.at[1])
    own_weight = pltpu.make_async_copy(weight_ref, weight.at[0], load_sem.at[3])
    own_weight.start()

    def norm(chunk):
        span = pl.ds(pl.multiple_of(chunk * step, step), step)
        x = values[span, :].astype(jnp.float32)
        inverse = lax.rsqrt(jnp.mean(x * x, axis=-1, keepdims=True) + epsilon)
        normed = x * inverse
        upstream = branch[span, :].astype(jnp.float32)
        scaled = upstream * gain[...]
        project = jnp.mean(scaled * normed, axis=-1, keepdims=True)
        boundary_out[span, :] = (
            residual[span, :].astype(jnp.float32)
            + inverse * (scaled - normed * project)
        ).astype(boundary_out.dtype)
        gain_sum[0] += jnp.sum(upstream * normed, axis=0, keepdims=True)

    def section_copy(chunk):
        span = pl.ds(pl.multiple_of(chunk * step, step), step)
        return remote(
            boundary_out.at[span],
            acts.at[span],
            by_section,
            section_recv.at[chunk],
            partner,
        )

    half = units // 2
    passed = half // 2
    first = passed - 16
    more = (half // 7 // 16) * 16
    shared = passed - more

    def from_edge(side, near, far, size):
        which = me_twin + side - 2 * me_twin * side
        start = me_core * half + near + which * (far - near)
        return pl.ds(pl.multiple_of(start, 16), size)

    sides = range(2)
    parts = (0, first), (first, passed - first)
    going = [from_edge(side, 0, half - passed, passed) for side in sides]
    going_parts = [
        [from_edge(side, at, half - passed + at, size) for side in sides]
        for at, size in parts
    ]
    extra = [from_edge(side, passed, half - passed - more, more) for side in sides]
    given = [from_edge(side, 0, half - shared, shared) for side in sides]
    gotten = [from_edge(side, half - shared, 0, shared) for side in sides]
    slots = (3, 1)
    ways = (up, down)

    def from_home(i, side, span):
        return remote(
            weight_ref.at[span],
            weight.at[slots[side], span],
            by_weight,
            row_recv.at[i],
            ways[side],
        )

    def onward(i, side, span):
        return remote(
            weight.at[slots[side], span],
            weight.at[2, span],
            by_weight,
            row_recv.at[i],
            ways[side],
        )

    def same_place(slot, span, device, receive):
        there = weight.at[slot, span]
        return remote(there, there, by_weight, receive, device)

    own_copies = [
        [from_home(2 * n + side, side, going_parts[n][side]) for side in sides]
        for n in range(2)
    ]
    extra_copies = [from_home(4 + side, side, extra[side]) for side in sides]
    pass_copies = [
        [onward(6 + 2 * n + side, side, going_parts[n][side]) for side in sides]
        for n in range(2)
    ]
    core_own = [
        same_place(slots[side], going[side], core, core_recv.at[side])
        for side in sides
    ]
    core_extra = [
        same_place(slots[side], extra[side], core, core_recv.at[2 + side])
        for side in sides
    ]
    core_gotten = [
        same_place(slots[side], gotten[side], core, core_recv.at[4 + side])
        for side in sides
    ]
    core_passed = [
        [
            same_place(2, going_parts[n][side], core, core_recv.at[6 + 2 * n + side])
            for side in sides
        ]
        for n in range(2)
    ]
    twin_given = [
        same_place(slots[side], given[side], twin, twin_recv.at[side])
        for side in sides
    ]

    def gain_copy(i):
        return remote(
            gain_sum.at[i], gain_in.at[i], by_gain, gain_recv.at[i], gain_partners[i]
        )

    def gain_step(i):
        gain_copy(i).wait_recv()
        gain_sum[i + 1] = gain_sum[i] + gain_in[i]
        if i + 1 < len(gain_partners):
            gain_copy(i + 1).start()

    pieces = CHUNKS // 2

    def ring_copy(way, hop, piece):
        size = step if hop == 1 else 2 * step
        here = first_row(rows, hop - 1, way) + piece * size
        there = first_row(rows, hop, way) + piece * size
        index = piece if hop == 1 else CHUNKS + (hop - 2) * pieces + piece
        return remote(
            acts.at[pl.ds(here, size)],
            acts.at[pl.ds(there, size)],
            by_ring + way,
            ring_recv.at[way, index],
            (right, left)[way],
        )

    def on_ring(way, hop, piece):
        return hop < 4 or (hop == 4 and piece % 2 == way)

    def from_section(chunk):
        section_copy(chunk).wait_recv()
        for way in range(2):
            ring_copy(way, 1, chunk).start()

    def hear(hop, *some):
        for piece in some:
            for way in range(2):
                if on_ring(way, hop, piece):
                    ring_copy(way, hop, piece).wait_recv()

    def pass_on(hop, *some):
        for piece in some:
            for way in range(2):
                if on_ring(way, hop + 1, piece):
                    ring_copy(way, hop + 1, piece).start()

    def tokens_of(origin):
        return pl.ds(pl.multiple_of(me_x * (8 * rows) + origin * rows, rows), rows)

    def origins(hop):
        if hop == 0:
            return ((0, me_z),)
        if hop == 4:
            return ((7, lax.rem(me_z + 4, 8)),)
        return (
            (2 * hop - 1, lax.rem(me_z + 8 - hop, 8)),
            (2 * hop, lax.rem(me_z + hop, 8)),
        )

    def product(hop, d):
        blocks = origins(hop)
        return lax.dot_general(
            weight[d],
            acts[pl.ds(blocks[0][0] * rows, rows * len(blocks)), :],
            (((1,), (1,)), ((), ())),
            preferred_element_type=jnp.float32,
        ).astype(result.dtype)

    def own_product(hop):
        found = product(hop, 0)
        for i, (_, origin) in enumerate(origins(hop)):
            unit_out[:, tokens_of(origin)] = found[:, i * rows : (i + 1) * rows]

    def sent_product(hop, d):
        found = product(hop, d)
        for i, (block, origin) in enumerate(origins(hop)):
            result[d - 1, block] = found[:, i * rows : (i + 1) * rows]
            remote(
                result.at[d - 1, block],
                unit_out.at[:, tokens_of(origin)],
                by_result + d - 1,
                result_recv.at[d - 1],
                {"shard_0": lax.rem(me_x + d, 4)},
            ).start()

    def side_products(hop):
        @pl.loop(0, 2)
        def _(i):
            sent_product(hop, 1 + 2 * i)

    def sent_products(hop):
        @pl.loop(0, 3)
        def _(i):
            sent_product(hop, 2 - i + 3 * (i // 2))

    gain_sum[0] = jnp.zeros_like(gain_sum[0])
    take(acts.at[pl.ds(0, 3 * step)], load_sem.at[0])
    gain_load.wait()
    norm(0)
    pl.semaphore_wait(barrier, len(others))
    section_copy(0).start()
    for copy in own_copies[0] + own_copies[1]:
        copy.start()
    take(acts.at[pl.ds(0, 3 * (rows - step))], load_sem.at[1])

    @pl.loop(1, CHUNKS)
    def _(chunk):
        norm(chunk)
        section_copy(chunk).start()

    gain_copy(0).start()

    for chunk in range(3):
        from_section(chunk)
    gain_step(0)
    from_section(3)
    from_section(4)
    gain_step(1)
    from_section(5)
    for side in sides:
        own_copies[0][side].wait_recv()
        pass_copies[0][side].start()
    from_section(6)
    from_section(7)
    for side in sides:
        own_copies[1][side].wait_recv()
        pass_copies[1][side].start()
        extra_copies[side].start()
        core_own[side].start()
        twin_given[side].start()
    hear(1, 0, 1, 2, 3, 4, 5)
    pass_on(1, 0, 1, 2)
    gain_step(2)
    hear(1, 6, 7)
    pass_on(1, 3)
    own_weight.wait()
    own_product(0)
    own_product(1)
    gain_step(3)
    hear(2, 0)
    pass_on(2, 0)
    for side in sides:
        pass_copies[0][side].wait_recv()
        core_passed[0][side].start()
    hear(2, 1)
    pass_on(2, 1)
    for side in sides:
        pass_copies[1][side].wait_recv()
        core_passed[1][side].start()
    for side in sides:
        core_passed[0][side].wait_recv()
        core_passed[1][side].wait_recv()
    sent_product(0, 2)
    hear(2, 2)
    pass_on(2, 2)
    sent_product(1, 2)
    for side in sides:
        extra_copies[side].wait_recv()
        core_extra[side].start()
    gain_step(4)
    hear(2, 3)
    pass_on(2, 3)
    sent_product(2, 2)
    for side in sides:
        twin_given[side].wait_recv()
        core_gotten[side].start()
    for side in sides:
        core_own[side].wait_recv()
        core_extra[side].wait_recv()
        core_gotten[side].wait_recv()
    side_products(0)
    hear(3, 0)
    pass_on(3, 0)
    side_products(1)
    hear(3, 1)
    pass_on(3, 1)
    side_products(2)
    own_product(2)
    gain_step(5)
    hear(3, 2)
    pass_on(3, 2)
    hear(3, 3)
    pass_on(3, 3)
    sent_products(3)
    own_product(3)
    gain_step(6)
    gain_out[...] = gain_sum[7] * (1.0 / (32 * rows))
    hear(4, 0, 1, 2, 3)
    sent_products(4)
    own_product(4)

    take(gain_in, send_sem.at[by_gain])
    take(acts.at[pl.ds(0, rows)], send_sem.at[by_section])
    for way in range(2):
        take(acts.at[pl.ds(0, 3 * rows + rows // 2)], send_sem.at[by_ring + way])
    take(weight.at[pl.ds(0, 3)], send_sem.at[by_weight])
    for d in (1, 2, 3):
        take(result.at[d - 1], send_sem.at[by_result + d - 1])
        take(result.at[d - 1], result_recv.at[d - 1])


def store(boundary_ref, gain_ref, unit_ref, boundary_out, gain_out, unit_out, sem):
    part = unit_ref.shape[0] // 4
    pairs = [
        (unit_ref.at[pl.ds(i * part, part)], unit_out.at[pl.ds(i * part, part)])
        for i in range(4)
    ] + [(boundary_ref, boundary_out), (gain_ref, gain_out)]
    copies = [
        pltpu.make_async_copy(source, target, sem.at[i])
        for i, (source, target) in enumerate(pairs)
    ]
    for copy in copies:
        copy.start()
    for copy in copies:
        copy.wait()


def per_device(norm_input, norm_gain, branch_grad, residual_grad, down_weight):
    rows, features = norm_input.shape[2:]
    units = down_weight.shape[1]
    anywhere = pl.BlockSpec(memory_space=pl.ANY)
    whole = pl.BlockSpec(memory_space=pltpu.VMEM)
    dma = pltpu.SemaphoreType.DMA
    block = pltpu.VMEM((rows, features), jnp.bfloat16)
    boundary, gain_grad, unit_grads = pl.pallas_call(
        kernel,
        out_shape=(
            block,
            pltpu.VMEM((1, features), jnp.float32),
            pltpu.VMEM((units, 32 * rows), jnp.bfloat16),
        ),
        in_specs=[anywhere] * 5,
        out_specs=(whole,) * 3,
        scratch_shapes=[
            block,
            block,
            block,
            pltpu.VMEM((1, features), jnp.float32),
            pltpu.VMEM((8 * rows, features), jnp.bfloat16),
            pltpu.VMEM((4, units, features), jnp.bfloat16),
            pltpu.VMEM((3, 8, units, rows), jnp.bfloat16),
            pltpu.VMEM((8, 1, features), jnp.float32),
            pltpu.VMEM((7, 1, features), jnp.float32),
            dma((4,)),
            dma((CHUNKS,)),
            dma((2, CHUNKS + 3 * (CHUNKS // 2))),
            dma((10,)),
            dma((10,)),
            dma((2,)),
            dma((3,)),
            dma((7,)),
            dma((8,)),
        ],
        compiler_params=pltpu.CompilerParams(
            collective_id=0, has_side_effects=True, vmem_limit_bytes=40 << 20
        ),
        cost_estimate=pl.CostEstimate(
            flops=2 * 8 * rows * 4 * units * features,
            bytes_accessed=16 << 20,
            transcendentals=rows,
        ),
        name="relay_backward",
    )(
        *(
            pltpu.with_memory_space_constraint(given, pltpu.HBM)
            for given in (
                norm_input[0, 0],
                norm_gain,
                branch_grad[0, 0],
                residual_grad[0, 0],
                down_weight[0],
            )
        )
    )
    boundary, gain_grad, unit_grads = pl.pallas_call(
        store,
        out_shape=tuple(
            jax.ShapeDtypeStruct(found.shape, found.dtype)
            for found in (boundary, gain_grad, unit_grads)
        ),
        in_specs=[whole] * 3,
        out_specs=(anywhere,) * 3,
        scratch_shapes=[dma((6,))],
        compiler_params=pltpu.CompilerParams(vmem_limit_bytes=1 << 20),
        name="store_results",
    )(
        *(
            pltpu.with_memory_space_constraint(found, pltpu.VMEM)
            for found in (boundary, gain_grad, unit_grads)
        )
    )
    return (boundary[None, None], gain_grad, unit_grads.T[None, None])


def solution(mesh):
    split = Mesh(
        mesh.devices.reshape(mesh.shape["section"], 2, 2, 4, 8),
        ("section", "dp_0", "dp_1", "shard_0", "shard_1"),
    )
    return jax.shard_map(
        per_device,
        mesh=split,
        in_specs=(
            P("section", DP, SHARD, None),
            P("section", None),
            P("section", DP, SHARD, None),
            P("section", DP, SHARD, None),
            P("section", SHARD, None),
        ),
        out_specs=(
            P("section", DP, SHARD, None),
            P("section", None),
            P("section", DP, None, SHARD),
        ),
        check_vma=False,
    )
```

```python
import functools

import jax
import jax.numpy as jnp
from jax import lax
from jax.experimental import pallas as pl
from jax.experimental.pallas import tpu as pltpu
from jax.sharding import Mesh
from jax.sharding import PartitionSpec as P

DP_SHARD = ("dp_0", "dp_1", "shard_0", "shard_1")
SHARD = ("shard_0", "shard_1")
DP = ("dp_0", "dp_1")
MESH = pl.DeviceIdType.MESH

epsilon = 1e-05

CHUNKS = 8


def wrap(axis, offset):
    size = lax.axis_size(axis)
    return {axis: lax.rem(lax.axis_index(axis) + (offset % size), size)}


def flip(axis, bit):
    me = lax.axis_index(axis)
    return {axis: me + bit - 2 * bit * lax.rem(me // bit, 2)}


def first_row(rows, hop, way):
    if hop == 0:
        return 0
    if hop == 4:
        return 7 * rows
    return rows * (1 + 2 * (hop - 1) + way)


def kernel(
    input_ref,
    gain_ref,
    branch_ref,
    residual_ref,
    weight_ref,
    boundary_out,
    gain_out,
    unit_out,
    values,
    branch,
    residual,
    gain,
    acts,
    weight,
    result,
    gain_sum,
    gain_in,
    load_sem,
    section_recv,
    ring_recv,
    row_recv,
    core_recv,
    twin_recv,
    result_recv,
    gain_recv,
    send_sem,
):
    rows, features = input_ref.shape
    units = weight_ref.shape[0]
    step = rows // CHUNKS
    me_x = lax.axis_index("shard_0")
    me_z = lax.axis_index("shard_1")
    me_twin = lax.axis_index("dp_0")
    me_core = lax.axis_index("dp_1")

    right, left = wrap("shard_1", 1), wrap("shard_1", -1)
    up, down = wrap("shard_0", 1), wrap("shard_0", -1)
    partner, twin, core = wrap("section", 1), wrap("dp_0", 1), wrap("dp_1", 1)
    gain_partners = (
        flip("shard_1", 1),
        flip("shard_1", 2),
        wrap("shard_1", 4),
        core,
        flip("shard_0", 1),
        wrap("shard_0", 2),
        twin,
    )
    by_ring, by_section, by_weight, by_result, by_gain = 0, 2, 3, 4, 7

    def remote(source, target, send, receive, device):
        return pltpu.make_async_remote_copy(
            src_ref=source,
            dst_ref=target,
            send_sem=send_sem.at[send],
            recv_sem=receive,
            device_id=device,
            device_id_type=MESH,
        )

    def take(like, sem):
        pltpu.make_async_copy(like, like, sem).wait()

    def load(start, size, sem):
        span = pl.ds(start, size)
        for ref, buffer in (
            (input_ref, values),
            (branch_ref, branch),
            (residual_ref, residual),
        ):
            pltpu.make_async_copy(ref.at[span], buffer.at[span], sem).start()

    load(0, step, load_sem.at[0])
    gain_load = pltpu.make_async_copy(gain_ref, gain, load_sem.at[2])
    gain_load.start()

    barrier = pltpu.get_barrier_semaphore()
    others = (
        right,
        left,
        flip("shard_1", 2),
        wrap("shard_1", 4),
        up,
        down,
        wrap("shard_0", 2),
        partner,
        twin,
        core,
    )
    for other in others:
        pl.semaphore_signal(barrier, inc=1, device_id=other, device_id_type=MESH)
    load(step, rows - step, load_sem.at[1])
    own_weight = pltpu.make_async_copy(weight_ref, weight.at[0], load_sem.at[3])
    own_weight.start()

    def norm(chunk):
        span = pl.ds(pl.multiple_of(chunk * step, step), step)
        x = values[span, :].astype(jnp.float32)
        inverse = lax.rsqrt(jnp.mean(x * x, axis=-1, keepdims=True) + epsilon)
        normed = x * inverse
        upstream = branch[span, :].astype(jnp.float32)
        scaled = upstream * gain[...]
        project = jnp.mean(scaled * normed, axis=-1, keepdims=True)
        boundary_out[span, :] = (
            residual[span, :].astype(jnp.float32)
            + inverse * (scaled - normed * project)
        ).astype(boundary_out.dtype)
        gain_sum[0] += jnp.sum(upstream * normed, axis=0, keepdims=True)

    def section_copy(chunk):
        span = pl.ds(pl.multiple_of(chunk * step, step), step)
        return remote(
            boundary_out.at[span],
            acts.at[span],
            by_section,
            section_recv.at[chunk],
            partner,
        )

    half = units // 2
    passed = half // 2
    first = passed - 16
    more = (half // 7 // 16) * 16
    shared = passed - more

    def from_edge(side, near, far, size):
        which = me_twin + side - 2 * me_twin * side
        start = me_core * half + near + which * (far - near)
        return pl.ds(pl.multiple_of(start, 16), size)

    sides = range(2)
    parts = (0, first), (first, passed - first)
    going = [from_edge(side, 0, half - passed, passed) for side in sides]
    going_parts = [
        [from_edge(side, at, half - passed + at, size) for side in sides]
        for at, size in parts
    ]
    extra = [from_edge(side, passed, half - passed - more, more) for side in sides]
    given = [from_edge(side, 0, half - shared, shared) for side in sides]
    gotten = [from_edge(side, half - shared, 0, shared) for side in sides]
    slots = (3, 1)
    ways = (up, down)

    def from_home(i, side, span):
        return remote(
            weight_ref.at[span],
            weight.at[slots[side], span],
            by_weight,
            row_recv.at[i],
            ways[side],
        )

    def onward(i, side, span):
        return remote(
            weight.at[slots[side], span],
            weight.at[2, span],
            by_weight,
            row_recv.at[i],
            ways[side],
        )

    def same_place(slot, span, device, receive):
        there = weight.at[slot, span]
        return remote(there, there, by_weight, receive, device)

    own_copies = [
        [from_home(n, side, going_parts[n][side]) for side in sides]
        for n in range(2)
    ]
    extra_copies = [from_home(2, side, extra[side]) for side in sides]
    pass_copies = [
        [onward(3 + n, side, going_parts[n][side]) for side in sides]
        for n in range(2)
    ]
    core_own = [
        same_place(slots[side], going[side], core, core_recv.at[0])
        for side in sides
    ]
    core_extra = [
        same_place(slots[side], extra[side], core, core_recv.at[1])
        for side in sides
    ]
    core_gotten = [
        same_place(slots[side], gotten[side], core, core_recv.at[2])
        for side in sides
    ]
    core_passed = [
        [
            same_place(2, going_parts[n][side], core, core_recv.at[3 + n])
            for side in sides
        ]
        for n in range(2)
    ]
    twin_given = [
        same_place(slots[side], given[side], twin, twin_recv.at[0])
        for side in sides
    ]

    def both(size, sem):
        take(acts.at[pl.ds(0, 2 * size)], sem)

    def gain_copy(i):
        return remote(
            gain_sum.at[i], gain_in.at[i], by_gain, gain_recv.at[i], gain_partners[i]
        )

    def gain_step(i):
        gain_copy(i).wait_recv()
        gain_sum[i + 1] = gain_sum[i] + gain_in[i]
        if i + 1 < len(gain_partners):
            gain_copy(i + 1).start()

    pieces = CHUNKS // 2

    def ring_index(hop, piece):
        return piece if hop == 1 else CHUNKS + (hop - 2) * pieces + piece

    def ring_copy(way, hop, piece):
        size = step if hop == 1 else 2 * step
        here = first_row(rows, hop - 1, way) + piece * size
        there = first_row(rows, hop, way) + piece * size
        index = ring_index(hop, piece)
        return remote(
            acts.at[pl.ds(here, size)],
            acts.at[pl.ds(there, size)],
            by_ring + way,
            ring_recv.at[index],
            (right, left)[way],
        )

    def on_ring(way, hop, piece):
        return hop < 4 or (hop == 4 and piece % 2 == way)

    def from_section(chunk):
        section_copy(chunk).wait_recv()
        for way in range(2):
            ring_copy(way, 1, chunk).start()

    def hear(hop, *some):
        size = step if hop == 1 else 2 * step
        for piece in some:
            arrive = sum(on_ring(way, hop, piece) for way in range(2))
            take(
                acts.at[pl.ds(0, arrive * size)],
                ring_recv.at[ring_index(hop, piece)],
            )

    def pass_on(hop, *some):
        for piece in some:
            for way in range(2):
                if on_ring(way, hop + 1, piece):
                    ring_copy(way, hop + 1, piece).start()

    def tokens_of(origin):
        return pl.ds(pl.multiple_of(me_x * (8 * rows) + origin * rows, rows), rows)

    def origins(hop):
        if hop == 0:
            return ((0, me_z),)
        if hop == 4:
            return ((7, lax.rem(me_z + 4, 8)),)
        return (
            (2 * hop - 1, lax.rem(me_z + 8 - hop, 8)),
            (2 * hop, lax.rem(me_z + hop, 8)),
        )

    def product(hop, d):
        blocks = origins(hop)
        return lax.dot_general(
            weight[d],
            acts[pl.ds(blocks[0][0] * rows, rows * len(blocks)), :],
            (((1,), (1,)), ((), ())),
            preferred_element_type=jnp.float32,
        ).astype(result.dtype)

    def own_product(hop):
        found = product(hop, 0)
        for i, (_, origin) in enumerate(origins(hop)):
            unit_out[:, tokens_of(origin)] = found[:, i * rows : (i + 1) * rows]

    def sent_product(hop, d):
        found = product(hop, d)
        for i, (block, origin) in enumerate(origins(hop)):
            result[d - 1, block] = found[:, i * rows : (i + 1) * rows]
            remote(
                result.at[d - 1, block],
                unit_out.at[:, tokens_of(origin)],
                by_result + d - 1,
                result_recv.at[d - 1],
                {"shard_0": lax.rem(me_x + d, 4)},
            ).start()

    def side_products(hop):
        @pl.loop(0, 2)
        def _(i):
            sent_product(hop, 1 + 2 * i)

    def sent_products(hop):
        @pl.loop(0, 3)
        def _(i):
            sent_product(hop, 2 - i + 3 * (i // 2))

    gain_sum[0] = jnp.zeros_like(gain_sum[0])
    take(acts.at[pl.ds(0, 3 * step)], load_sem.at[0])
    gain_load.wait()
    norm(0)
    pl.semaphore_wait(barrier, len(others))
    section_copy(0).start()
    for copy in own_copies[0] + own_copies[1]:
        copy.start()
    take(acts.at[pl.ds(0, 3 * (rows - step))], load_sem.at[1])

    @pl.loop(1, CHUNKS)
    def _(chunk):
        norm(chunk)
        section_copy(chunk).start()

    gain_copy(0).start()

    for chunk in range(3):
        from_section(chunk)
    gain_step(0)
    from_section(3)
    from_section(4)
    gain_step(1)
    from_section(5)
    both(first, row_recv.at[0])
    for side in sides:
        pass_copies[0][side].start()
    from_section(6)
    from_section(7)
    both(passed - first, row_recv.at[1])
    for side in sides:
        pass_copies[1][side].start()
        extra_copies[side].start()
        core_own[side].start()
        twin_given[side].start()
    hear(1, 0, 1, 2, 3, 4, 5)
    pass_on(1, 0, 1, 2)
    gain_step(2)
    hear(1, 6, 7)
    pass_on(1, 3)
    own_weight.wait()
    own_product(0)
    own_product(1)
    gain_step(3)
    hear(2, 0)
    pass_on(2, 0)
    both(first, row_recv.at[3])
    for side in sides:
        core_passed[0][side].start()
    hear(2, 1)
    pass_on(2, 1)
    both(passed - first, row_recv.at[4])
    for side in sides:
        core_passed[1][side].start()
    both(first, core_recv.at[3])
    both(passed - first, core_recv.at[4])
    sent_product(0, 2)
    hear(2, 2)
    pass_on(2, 2)
    sent_product(1, 2)
    both(more, row_recv.at[2])
    for side in sides:
        core_extra[side].start()
    gain_step(4)
    hear(2, 3)
    pass_on(2, 3)
    sent_product(2, 2)
    both(shared, twin_recv.at[0])
    for side in sides:
        core_gotten[side].start()
    both(passed, core_recv.at[0])
    both(more, core_recv.at[1])
    both(shared, core_recv.at[2])
    side_products(0)
    hear(3, 0)
    pass_on(3, 0)
    side_products(1)
    hear(3, 1)
    pass_on(3, 1)
    side_products(2)
    own_product(2)
    gain_step(5)
    hear(3, 2)
    pass_on(3, 2)
    hear(3, 3)
    pass_on(3, 3)
    sent_products(3)
    own_product(3)
    gain_step(6)
    gain_out[...] = gain_sum[7] * (1.0 / (32 * rows))
    hear(4, 0, 1, 2, 3)
    sent_products(4)
    own_product(4)

    take(gain_in, send_sem.at[by_gain])
    take(acts.at[pl.ds(0, rows)], send_sem.at[by_section])
    for way in range(2):
        take(acts.at[pl.ds(0, 3 * rows + rows // 2)], send_sem.at[by_ring + way])
    take(weight.at[pl.ds(0, 3)], send_sem.at[by_weight])
    for d in (1, 2, 3):
        take(result.at[d - 1], send_sem.at[by_result + d - 1])
        take(result.at[d - 1], result_recv.at[d - 1])


def store(boundary_ref, gain_ref, unit_ref, boundary_out, gain_out, unit_out, sem):
    part = unit_ref.shape[0] // 4
    pairs = [
        (unit_ref.at[pl.ds(i * part, part)], unit_out.at[pl.ds(i * part, part)])
        for i in range(4)
    ] + [(boundary_ref, boundary_out), (gain_ref, gain_out)]
    copies = [
        pltpu.make_async_copy(source, target, sem.at[i])
        for i, (source, target) in enumerate(pairs)
    ]
    for copy in copies:
        copy.start()
    for copy in copies:
        copy.wait()


def per_device(norm_input, norm_gain, branch_grad, residual_grad, down_weight):
    rows, features = norm_input.shape[2:]
    units = down_weight.shape[1]
    anywhere = pl.BlockSpec(memory_space=pl.ANY)
    whole = pl.BlockSpec(memory_space=pltpu.VMEM)
    dma = pltpu.SemaphoreType.DMA
    block = pltpu.VMEM((rows, features), jnp.bfloat16)
    boundary, gain_grad, unit_grads = pl.pallas_call(
        kernel,
        out_shape=(
            block,
            pltpu.VMEM((1, features), jnp.float32),
            pltpu.VMEM((units, 32 * rows), jnp.bfloat16),
        ),
        in_specs=[anywhere] * 5,
        out_specs=(whole,) * 3,
        scratch_shapes=[
            block,
            block,
            block,
            pltpu.VMEM((1, features), jnp.float32),
            pltpu.VMEM((8 * rows, features), jnp.bfloat16),
            pltpu.VMEM((4, units, features), jnp.bfloat16),
            pltpu.VMEM((3, 8, units, rows), jnp.bfloat16),
            pltpu.VMEM((8, 1, features), jnp.float32),
            pltpu.VMEM((7, 1, features), jnp.float32),
            dma((4,)),
            dma((CHUNKS,)),
            dma((CHUNKS + 3 * (CHUNKS // 2),)),
            dma((5,)),
            dma((5,)),
            dma((1,)),
            dma((3,)),
            dma((7,)),
            dma((8,)),
        ],
        compiler_params=pltpu.CompilerParams(
            collective_id=0, has_side_effects=True, vmem_limit_bytes=40 << 20
        ),
        cost_estimate=pl.CostEstimate(
            flops=2 * 8 * rows * 4 * units * features,
            bytes_accessed=16 << 20,
            transcendentals=rows,
        ),
        name="relay_backward",
    )(
        *(
            pltpu.with_memory_space_constraint(given, pltpu.HBM)
            for given in (
                norm_input[0, 0],
                norm_gain,
                branch_grad[0, 0],
                residual_grad[0, 0],
                down_weight[0],
            )
        )
    )
    boundary, gain_grad, unit_grads = pl.pallas_call(
        store,
        out_shape=tuple(
            jax.ShapeDtypeStruct(found.shape, found.dtype)
            for found in (boundary, gain_grad, unit_grads)
        ),
        in_specs=[whole] * 3,
        out_specs=(anywhere,) * 3,
        scratch_shapes=[dma((6,))],
        compiler_params=pltpu.CompilerParams(vmem_limit_bytes=1 << 20),
        name="store_results",
    )(
        *(
            pltpu.with_memory_space_constraint(found, pltpu.VMEM)
            for found in (boundary, gain_grad, unit_grads)
        )
    )
    return (boundary[None, None], gain_grad, unit_grads.T[None, None])


def solution(mesh):
    split = Mesh(
        mesh.devices.reshape(mesh.shape["section"], 2, 2, 4, 8),
        ("section", "dp_0", "dp_1", "shard_0", "shard_1"),
    )
    return jax.shard_map(
        per_device,
        mesh=split,
        in_specs=(
            P("section", DP, SHARD, None),
            P("section", None),
            P("section", DP, SHARD, None),
            P("section", DP, SHARD, None),
            P("section", SHARD, None),
        ),
        out_specs=(
            P("section", DP, SHARD, None),
            P("section", None),
            P("section", DP, None, SHARD),
        ),
        check_vma=False,
    )
```
